32 devices in a mesh: px: 16 (over z, x, core), pz: 2 (over y).
Axes of the slice: x: 2, y: 2, z: 4, core: 2. Of those that a mesh axis runs over, the one named last changes fastest.
Arguments:
- base: float32 [3, 256, 256, 128], P(None, 'px', 'pz'), may hold values from -6 to 6
- adjoint: float32 [3, 256, 256, 128], P(None, 'px', 'pz'), may hold values from -6 to 6
- tangent: float32 [1, 3, 256, 256, 128], P(None, None, 'px', 'pz'), may hold values from -6 to 6
- second: float32 [1, 3, 256, 256, 128], P(None, None, 'px', 'pz'), may hold values from -6 to 6
- dealias_mask: int32 [256, 256], P('px', 'pz'), may hold values 0 or 1
- tau_rows: int32 [256, 256, 2], P('px', 'pz'), may hold values from 0 to 63
- tau_inverse: float32 [256, 256, 64, 128], P('px', 'pz'), may hold values from -1 to 2.5, as said below
Outputs:
- base_next: float32 [3, 256, 256, 128], P(None, 'px', 'pz')
- adjoint_next: float32 [3, 256, 256, 128], P(None, 'px', 'pz')
- tangent_next: float32 [1, 3, 256, 256, 128], P(None, None, 'px', 'pz')
- second_next: float32 [1, 3, 256, 256, 128], P(None, None, 'px', 'pz')
The draws below stay inside these ranges and needn't reach their ends.
Inputs may be any that keep to these rules, and one draw needn't show every extreme that they name: `tau_inverse`: entry [kx, kz, a, p * 64 + b] maps the input at Chebyshev index 2 b + p to the output at index 2 a + p.
All inputs are finite; a program needn't handle non-finite values. No bound on the sum of `dealias_mask` on one device may be relied on, other than what follows from the above.
Results may differ from the reference program's by a relative error of at most 0.00013.
Values sent between devices are 32-bit elements; how exact they have to be, the bound alone decides.
A program may use at most 256 MiB of HBM per device.

```python
import math
import jax
import jax.numpy as jnp
from jax import lax

NX = 256
NZ = 256
NY = 128
DIRS = 1
HALF = 64


def draw_tau_inverse(key, part):
    shape = (NX, NZ, HALF, NY)
    key_noise = jax.random.fold_in(key, 11)
    key_diag = jax.random.fold_in(key, 23)
    spread = 0.6 / math.sqrt(HALF)
    noise = jnp.clip(jax.random.normal(key_noise, shape, jnp.float32), -4.0, 4.0) * spread
    diagonal = jax.random.uniform(key_diag, (NX, NZ, HALF, 2), jnp.float32, 0.5, 1.5)
    diagonal_full = jnp.repeat(diagonal, HALF, axis=3)
    outputs = jnp.arange(HALF, dtype=jnp.int32)[:, None]
    columns = jnp.arange(NY, dtype=jnp.int32)[None, :] % HALF
    identity = (outputs == columns)[None, None]
    return noise + jnp.where(identity, diagonal_full, jnp.zeros_like(diagonal_full))


def place_ends(array, key, least, top_value):
    spot = [jax.random.randint(jax.random.fold_in(key, axis), (), 0, length) for axis, length in enumerate(array.shape)]
    longest = array.shape.index(max(array.shape))
    beside = spot[:longest] + [(spot[longest] + 1) % array.shape[longest]] + spot[longest + 1:]
    return array.at[tuple(spot)].set(least).at[tuple(beside)].set(top_value)


def shard_levels(key, dims, cuts, smallest, top_value):
    factor_of, own = 1.0, jax.random.fold_in(key, 6)
    for position, shards_of in cuts:
        heights = jnp.exp(jax.random.uniform(jax.random.fold_in(own, position), (shards_of,), jnp.float32, smallest / len(cuts), top_value / len(cuts)))
        factor_of = factor_of * jnp.repeat(heights, dims[position] // shards_of).reshape([-1 if axis == position else 1 for axis in range(len(dims))])
    return factor_of


def gaussian(key, shape, scale, bound, split=(), held_as=jnp.bfloat16):
    values = scale * jax.random.normal(key, shape, jnp.float32)
    if split:
        values = values * shard_levels(key, shape, split, -0.22, 0.18)
    return jnp.clip(values, -bound, bound).astype(held_as)


def setup_inputs(seed: int = 0) -> dict:
    splits = jax.random.split(jax.random.key(seed), 8)
    base = gaussian(splits[0], (3, NX, NZ, NY), 1.0, 6.0, ((1, 16), (2, 2)), jnp.float32)
    adjoint = gaussian(splits[1], (3, NX, NZ, NY), 1.0, 6.0, ((1, 16), (2, 2)), jnp.float32)
    tangent = gaussian(splits[2], (DIRS, 3, NX, NZ, NY), 1.0, 6.0, ((2, 16), (3, 2)), jnp.float32)
    second = gaussian(splits[3], (DIRS, 3, NX, NZ, NY), 1.0, 6.0, ((2, 16), (3, 2)), jnp.float32)
    dealias_mask = place_ends((jax.random.randint(splits[4], (NX, NZ), 0, 3) < 2).astype(jnp.int32), jax.random.fold_in(splits[4], 1), 0, 1)
    tau_rows = place_ends(jax.random.randint(splits[5], (NX, NZ, 2), 0, HALF), jax.random.fold_in(splits[5], 1), 0, HALF - 1).astype(jnp.int32)
    tau_inverse = draw_tau_inverse(jax.random.fold_in(splits[7], 71), 0)
    return dict(base=base, adjoint=adjoint, tangent=tangent, second=second, dealias_mask=dealias_mask, tau_rows=tau_rows, tau_inverse=tau_inverse)


step_gain = 0.5

def hartley(length):
    indices = jnp.arange(length, dtype=jnp.int32)
    product = indices[:, None] * indices[None, :] % length
    angles = product.astype(jnp.float32) * (2.0 * math.pi / length)
    return (jnp.cos(angles) + jnp.sin(angles)) / math.sqrt(length)

def hartley_slope(length):
    indices = jnp.arange(length, dtype=jnp.int32)
    product = indices[:, None] * indices[None, :] % length
    angles = product.astype(jnp.float32) * (2.0 * math.pi / length)
    signed = jnp.where(indices < length // 2, indices, indices - length).astype(jnp.float32)
    return (jnp.cos(angles) - jnp.sin(angles)) * (signed * (2.0 * math.pi / length))[None, :] / math.sqrt(length)

def chebyshev(length):
    indices = jnp.arange(length, dtype=jnp.int32)
    product = (2 * indices[:, None] + 1) * indices[None, :] % (4 * length)
    angles = product.astype(jnp.float32) * (math.pi / (2 * length))
    column_scale = jnp.where(indices == 0, math.sqrt(1.0 / length), math.sqrt(2.0 / length)).astype(jnp.float32)
    return jnp.cos(angles) * column_scale[None, :]

def chebyshev_slope(length):
    indices = jnp.arange(length, dtype=jnp.int32)
    product = (2 * indices[:, None] + 1) * indices[None, :] % (4 * length)
    angles = product.astype(jnp.float32) * (math.pi / (2 * length))
    nodes = jnp.sin((2 * indices + 1).astype(jnp.float32) * (math.pi / (2 * length)))
    column_scale = jnp.where(indices == 0, math.sqrt(1.0 / length), math.sqrt(2.0 / length)).astype(jnp.float32)
    column_scale = column_scale * indices.astype(jnp.float32)
    return jnp.sin(angles) * column_scale[None, :] / (length * nodes[:, None])

def crossed(first, other, axis):
    return jnp.roll(first, -1, axis) * jnp.roll(other, -2, axis) - jnp.roll(first, -2, axis) * jnp.roll(other, -1, axis)

def forcings(velocity, vortex):
    grid_shape = velocity.shape[2:]
    base_v, adj_v = (velocity[0], velocity[1])
    tang_v, sec_v = (velocity[2:2 + DIRS], velocity[2 + DIRS:])
    base_o, adj_o = (vortex[0], vortex[1])
    tang_o, sec_o = (vortex[2:2 + DIRS], vortex[2 + DIRS:])
    force_base = crossed(base_v, base_o, 0)
    force_adjoint = crossed(base_v, adj_o, 0) + crossed(adj_v, base_o, 0)
    force_tangent = crossed(base_v[None], tang_o, 1) + crossed(tang_v, base_o[None], 1)
    force_second = crossed(base_v[None], sec_o, 1) + crossed(sec_v, base_o[None], 1) + crossed(tang_v, adj_o[None], 1) + crossed(adj_v[None], tang_o, 1)
    return jnp.concatenate([force_base, force_adjoint, force_tangent.reshape((3 * DIRS,) + grid_shape), force_second.reshape((3 * DIRS,) + grid_shape)], 0)

def to_physical(stacked, table_x, table_z, table_y):
    highest = lax.Precision.HIGHEST
    result = jnp.einsum('cxzn,jn->cxzj', stacked, table_y, precision=highest)
    result = jnp.einsum('cxkj,zk->cxzj', result, table_z, precision=highest)
    return jnp.einsum('ckzj,xk->cxzj', result, table_x, precision=highest)

def reference(base, adjoint, tangent, second, dealias_mask, tau_rows, tau_inverse):
    highest = lax.Precision.HIGHEST
    grid_shape = (NX, NZ, NY)
    count = 2 + 2 * DIRS
    hart_x = hartley(NX)
    hart_z = hartley(NZ)
    cheb_y = chebyshev(NY)
    stacked = jnp.concatenate([base, adjoint, tangent.reshape((3 * DIRS,) + grid_shape), second.reshape((3 * DIRS,) + grid_shape)], 0)
    fields = stacked.shape[0]
    values = to_physical(stacked, hart_x, hart_z, cheb_y).reshape((count, 3) + grid_shape)
    slope_x = to_physical(stacked, hartley_slope(NX), hart_z, cheb_y).reshape((count, 3) + grid_shape)
    slope_z = to_physical(stacked, hart_x, hartley_slope(NZ), cheb_y).reshape((count, 3) + grid_shape)
    slope_y = to_physical(stacked, hart_x, hart_z, chebyshev_slope(NY)).reshape((count, 3) + grid_shape)
    vortex = jnp.stack([slope_y[:, 2] - slope_z[:, 1], slope_z[:, 0] - slope_x[:, 2], slope_x[:, 1] - slope_y[:, 0]], 1)
    forcing = forcings(values, vortex)
    spectral = jnp.einsum('cxzj,xk->ckzj', forcing, hart_x, precision=highest)
    spectral = jnp.einsum('cxzj,zk->cxkj', spectral, hart_z, precision=highest)
    forcing_hat = jnp.einsum('cxzj,jn->cxzn', spectral, cheb_y, precision=highest)
    right_side = stacked + step_gain * forcing_hat * dealias_mask.astype(jnp.float32)[None, :, :, None]
    right_side = right_side.reshape((fields, NX, NZ, HALF, 2))
    kept_rows = jnp.arange(HALF, dtype=jnp.int32)[None, None, :, None] != tau_rows[:, :, None, :]
    right_side = jnp.where(kept_rows[None], right_side, jnp.zeros_like(right_side))
    blocks = tau_inverse.reshape((NX, NZ, HALF, 2, HALF))

    def solve_line(pieces):
        return jnp.einsum('zapb,czbp->czap', pieces[0], pieces[1], precision=highest)
    solved = lax.map(solve_line, (blocks, jnp.moveaxis(right_side, 1, 0)))
    solved = jnp.moveaxis(solved, 0, 1).reshape((fields,) + grid_shape)
    base_next = solved[0:3]
    adjoint_next = solved[3:6]
    tangent_next = solved[6:6 + 3 * DIRS].reshape((DIRS, 3) + grid_shape)
    second_next = solved[6 + 3 * DIRS:].reshape((DIRS, 3) + grid_shape)
    return (base_next, adjoint_next, tangent_next, second_next)
```

```python
import math

import jax
import jax.numpy as jnp
from jax import lax
from jax.sharding import PartitionSpec as P

NX = 256
NZ = 256
NY = 128
DIRS = 1
HALF = 64


step_gain = 0.5


def hartley(length):
    indices = jnp.arange(length, dtype=jnp.int32)
    product = indices[:, None] * indices[None, :] % length
    angles = product.astype(jnp.float32) * (2.0 * math.pi / length)
    return (jnp.cos(angles) + jnp.sin(angles)) / math.sqrt(length)


def hartley_slope(length):
    indices = jnp.arange(length, dtype=jnp.int32)
    product = indices[:, None] * indices[None, :] % length
    angles = product.astype(jnp.float32) * (2.0 * math.pi / length)
    signed = jnp.where(indices < length // 2, indices, indices - length).astype(jnp.float32)
    return (
        (jnp.cos(angles) - jnp.sin(angles))
        * (signed * (2.0 * math.pi / length))[None, :]
        / math.sqrt(length)
    )


def chebyshev(length):
    indices = jnp.arange(length, dtype=jnp.int32)
    product = (2 * indices[:, None] + 1) * indices[None, :] % (4 * length)
    angles = product.astype(jnp.float32) * (math.pi / (2 * length))
    column_scale = jnp.where(indices == 0, math.sqrt(1.0 / length), math.sqrt(2.0 / length)).astype(
        jnp.float32
    )
    return jnp.cos(angles) * column_scale[None, :]


def chebyshev_slope(length):
    indices = jnp.arange(length, dtype=jnp.int32)
    product = (2 * indices[:, None] + 1) * indices[None, :] % (4 * length)
    angles = product.astype(jnp.float32) * (math.pi / (2 * length))
    nodes = jnp.sin((2 * indices + 1).astype(jnp.float32) * (math.pi / (2 * length)))
    column_scale = jnp.where(indices == 0, math.sqrt(1.0 / length), math.sqrt(2.0 / length)).astype(
        jnp.float32
    )
    column_scale = column_scale * indices.astype(jnp.float32)
    return jnp.sin(angles) * column_scale[None, :] / (length * nodes[:, None])


def crossed(first, other, axis):
    return jnp.roll(first, -1, axis) * jnp.roll(other, -2, axis) - jnp.roll(
        first, -2, axis
    ) * jnp.roll(other, -1, axis)


def forcings(velocity, vortex):
    grid_shape = velocity.shape[2:]
    base_v, adj_v = (velocity[0], velocity[1])
    tang_v, sec_v = (velocity[2 : 2 + DIRS], velocity[2 + DIRS :])
    base_o, adj_o = (vortex[0], vortex[1])
    tang_o, sec_o = (vortex[2 : 2 + DIRS], vortex[2 + DIRS :])
    force_base = crossed(base_v, base_o, 0)
    force_adjoint = crossed(base_v, adj_o, 0) + crossed(adj_v, base_o, 0)
    force_tangent = crossed(base_v[None], tang_o, 1) + crossed(tang_v, base_o[None], 1)
    force_second = (
        crossed(base_v[None], sec_o, 1)
        + crossed(sec_v, base_o[None], 1)
        + crossed(tang_v, adj_o[None], 1)
        + crossed(adj_v[None], tang_o, 1)
    )
    return jnp.concatenate(
        [
            force_base,
            force_adjoint,
            force_tangent.reshape((3 * DIRS,) + grid_shape),
            force_second.reshape((3 * DIRS,) + grid_shape),
        ],
        0,
    )


def parity_order():
    columns = jnp.arange(NY, dtype=jnp.int32)
    return 2 * (columns % HALF) + columns // HALF


def parity_table():
    return (jnp.arange(NY, dtype=jnp.int32)[:, None] == parity_order()[None, :]).astype(jnp.float32)


def to_physical_pencil(along_y, slope_y, tables, local_x, local_z, precise):
    hart_x, hart_z, slope_xt, slope_zt = tables
    groups_x = lax.axis_size("px")
    groups_z = lax.axis_size("pz")
    count = along_y.shape[0] // 3
    block_y = NY // groups_x
    block_x = NX // groups_z
    width = block_y * local_z

    def to_xlines(array):
        lead = array.shape[0]
        array = array.reshape((lead, local_x, local_z, groups_x, block_y))
        return array.transpose(0, 3, 1, 4, 2).reshape((lead, groups_x * local_x, width))

    whole_x, slope_whole = (
        lax.all_to_all(to_xlines(along_y), "px", split_axis=1, concat_axis=1, tiled=True),
        lax.all_to_all(to_xlines(slope_y), "px", split_axis=1, concat_axis=1, tiled=True),
    )
    values = jnp.einsum("ckm,xk->cxm", whole_x, hart_x, precision=precise)
    values = values.reshape((count, 3, NX, width))
    planar = whole_x.reshape((count, 3, NX, width))[:, 1:3].reshape((2 * count, NX, width))
    dx = jnp.einsum("ckm,xk->cxm", planar, slope_xt, precision=precise).reshape(
        (count, 2, NX, width)
    )
    dy = jnp.einsum("ckm,xk->cxm", slope_whole, hart_x, precision=precise).reshape(
        (count, 2, NX, width)
    )
    partial_value = jnp.stack(
        [values[:, 0], values[:, 1], values[:, 2], dy[:, 1], -dx[:, 1], dx[:, 0] - dy[:, 0]], 1
    )
    partial_value = partial_value.reshape((6 * count, NX, width))
    received = lax.all_to_all(partial_value, "pz", split_axis=1, concat_axis=1, tiled=True)
    received = received.reshape((6 * count, groups_z, block_x, block_y, local_z))
    received = received.transpose(0, 2, 3, 1, 4).reshape((count, 6, block_x, block_y, NZ))
    velocity = jnp.einsum("vcxjk,zk->vcxjz", received[:, 0:3], hart_z, precision=precise)
    rotated = jnp.einsum("vcxjk,zk->vcxjz", received[:, 3:6], hart_z, precision=precise)
    slope_v = jnp.einsum("vxjk,zk->vxjz", received[:, 1], slope_zt, precision=precise)
    slope_u = jnp.einsum("vxjk,zk->vxjz", received[:, 0], slope_zt, precision=precise)
    vortex = jnp.stack([rotated[:, 0] - slope_v, rotated[:, 1] + slope_u, rotated[:, 2]], 1)
    force = forcings(velocity, vortex)
    fields = force.shape[0]
    returned = jnp.einsum("cxjz,zk->cxjk", force, hart_z, precision=precise)
    returned = returned.reshape((fields, block_x, block_y, groups_z, local_z))
    returned = returned.transpose(0, 3, 1, 2, 4).reshape((fields, NX, width))
    mixed = lax.all_to_all(returned, "pz", split_axis=1, concat_axis=1, tiled=True)
    spectral_x = jnp.einsum("cxm,xk->ckm", mixed, hart_x, precision=precise)
    whole_y = lax.all_to_all(spectral_x, "px", split_axis=1, concat_axis=1, tiled=True)
    whole_y = whole_y.reshape((fields, groups_x, local_x, block_y, local_z))
    return whole_y.transpose(1, 3, 0, 2, 4).reshape((NY, fields, local_x, local_z))


def through_slabs(lines, tables, local_x, local_z, precise):
    hart_x, hart_z, slope_xt, slope_zt = tables
    groups_x = lax.axis_size("px")
    groups_z = lax.axis_size("pz")
    block_y = NY // (groups_x * groups_z)
    lead = lines.shape[1]
    count = lead // 5
    moved = lax.all_to_all(lines, ("px", "pz"), split_axis=0, concat_axis=0, tiled=True)
    moved = moved.reshape((groups_x, groups_z, block_y, lead, local_x, local_z))
    moved = moved.transpose(2, 3, 0, 4, 1, 5).reshape((block_y, lead, NX, NZ))
    moved = moved.transpose(1, 0, 2, 3)
    planes = jnp.einsum("cjkz,xk->cjxz", moved, hart_x, precision=precise)
    planes = planes.reshape((5, count, block_y, NX, NZ))
    dx = jnp.einsum(
        "cjkz,xk->cjxz", moved[count : 3 * count], slope_xt, precision=precise
    ).reshape((2, count, block_y, NX, NZ))
    partial_vortex = jnp.stack([planes[4], -dx[1], dx[0] - planes[3]], 1)
    velocity = jnp.einsum("cvjxk,zk->vcjxz", planes[0:3], hart_z, precision=precise)
    rotated = jnp.einsum("vcjxk,zk->vcjxz", partial_vortex, hart_z, precision=precise)
    dz = jnp.einsum("cvjxk,zk->vcjxz", planes[0:2], slope_zt, precision=precise)
    vortex = jnp.stack(
        [rotated[:, 0] - dz[:, 1], rotated[:, 1] + dz[:, 0], rotated[:, 2]], 1
    )
    force = forcings(velocity, vortex)
    fields = force.shape[0]
    force = jnp.einsum("cjxz,zk->cjxk", force, hart_z, precision=precise)
    force = jnp.einsum("cjxz,xk->cjkz", force, hart_x, precision=precise)
    force = force.reshape((fields, block_y, groups_x, local_x, groups_z, local_z))
    force = force.transpose(2, 4, 1, 0, 3, 5).reshape((NY, fields, local_x, local_z))
    return lax.all_to_all(force, ("px", "pz"), split_axis=0, concat_axis=0, tiled=True)


def body(base, adjoint, tangent, second, dealias_mask, tau_rows, tau_inverse):
    precise = lax.Precision.HIGH
    local_x = base.shape[1]
    local_z = base.shape[2]
    local_shape = (local_x, local_z, NY)
    count = 2 + 2 * DIRS
    tables = (hartley(NX), hartley(NZ), hartley_slope(NX), hartley_slope(NZ))
    cheb_y = chebyshev(NY)
    slope_yt = chebyshev_slope(NY)
    stacked = jnp.concatenate(
        [
            base,
            adjoint,
            tangent.reshape((3 * DIRS,) + local_shape),
            second.reshape((3 * DIRS,) + local_shape),
        ],
        0,
    )
    fields = stacked.shape[0]
    by_velocity = stacked.reshape((count, 3) + local_shape)
    if NY % (lax.axis_size("px") * lax.axis_size("pz")) == 0:
        grouped = by_velocity.transpose(1, 0, 2, 3, 4).reshape(stacked.shape)
        along_y = jnp.einsum("cxzn,jn->jcxz", grouped, cheb_y, precision=precise)
        sideways = by_velocity.transpose(1, 0, 2, 3, 4)[0::2].reshape((2 * count,) + local_shape)
        slope_y = jnp.einsum("cxzn,jn->jcxz", sideways, slope_yt, precision=precise)
        lines = jnp.concatenate([along_y, slope_y], 1)
        whole_y = through_slabs(lines, tables, local_x, local_z, precise)
    else:
        sideways = by_velocity[:, 0::2].reshape((2 * count,) + local_shape)
        along_y = jnp.einsum("cxzn,jn->cxzj", stacked, cheb_y, precision=precise)
        slope_y = jnp.einsum("cxzn,jn->cxzj", sideways, slope_yt, precision=precise)
        whole_y = to_physical_pencil(along_y, slope_y, tables, local_x, local_z, precise)
    parity = parity_table()
    forcing_hat = jnp.einsum("jcxz,jq->cxzq", whole_y, chebyshev(NY)[:, parity_order()], precision=precise)
    sorted_side = jnp.einsum("cxzn,nq->cxzq", stacked, parity, precision=lax.Precision.HIGHEST)
    right_side = (
        sorted_side + step_gain * forcing_hat * dealias_mask.astype(jnp.float32)[None, :, :, None]
    )
    columns = jnp.arange(NY, dtype=jnp.int32)
    rows = jnp.where(columns < HALF, tau_rows[:, :, 0:1], tau_rows[:, :, 1:2])
    keep = rows != (columns % HALF)
    right_side = jnp.where(keep[None], right_side, 0.0)
    halves = (columns // HALF)[None, :] == jnp.arange(2, dtype=jnp.int32)[:, None]
    blocked = jnp.where(halves[None, :, None, None, :], right_side[:, None], 0.0)
    solved = jnp.einsum("xzaq,cpxzq->xzcpa", tau_inverse, blocked, precision=precise)
    places = parity.T.reshape((2, HALF, NY))
    solved = jnp.einsum(
        "xzca,an->cxzn", solved[:, :, :, 0], places[0], precision=lax.Precision.HIGHEST
    ) + jnp.einsum("xzca,an->cxzn", solved[:, :, :, 1], places[1], precision=lax.Precision.HIGHEST)
    base_next = solved[0:3]
    adjoint_next = solved[3:6]
    tangent_next = solved[6 : 6 + 3 * DIRS].reshape((DIRS, 3) + local_shape)
    second_next = solved[6 + 3 * DIRS :].reshape((DIRS, 3) + local_shape)
    return (base_next, adjoint_next, tangent_next, second_next)


def solution(mesh):
    in_specs = (
        P(None, "px", "pz", None),
        P(None, "px", "pz", None),
        P(None, None, "px", "pz", None),
        P(None, None, "px", "pz", None),
        P("px", "pz"),
        P("px", "pz", None),
        P("px", "pz", None, None),
    )
    out_specs = (
        P(None, "px", "pz", None),
        P(None, "px", "pz", None),
        P(None, None, "px", "pz", None),
        P(None, None, "px", "pz", None),
    )
    return jax.shard_map(body, mesh=mesh, in_specs=in_specs, out_specs=out_specs, check_vma=False)
```
